32 devices in a mesh: space: 4 (over y, x), mode: 8 (over z, core).
Axes of the slice: x: 2, y: 2, z: 4, core: 2. Of those that a mesh axis runs over, the one named last changes fastest.
Arguments:
- excess_phonon_enthalpy: bfloat16 [768, 32, 128, 128], P('mode', 'space'), may hold values from -0.21972656 to 0.21972656
- thermal_offset: float32 [128, 128, 32], P('space', 'mode'), may hold values from -6 to 6
- state_specific_warmth_scaled: float32 [768], P('mode'), may hold values from 0.5 to 2
- scattering_lifetimes: float32 [768], P('mode'), may hold values from 0.5 to 50
- state_polarization_label: int32 [768], P('mode'), may hold values from 0 to 5
- state_orientation_label: int32 [768], P('mode'), may hold values from 0 to 15
- polarization_propagation_rate: float32 [6], replicated, may hold values from 0.3 to 1
- thermal_conductance_bulk: float32 [128, 128, 32], P('space', 'mode'), may hold values from 0.25 to 1
- substance_label: int32 [128, 128, 32], P('space', 'mode'), may hold values 0 or 1
Outputs:
- final_temperature: float32 [128, 128, 32], P('space', 'mode')
- heat_flux: float32 [3, 128, 128, 32], P(None, 'space', 'mode')
The draws below stay inside these ranges and needn't reach their ends.
Inputs may be any that keep to these rules, and one draw needn't show every extreme that they name: `substance_label`: 1 marks a pore cell.
All inputs are finite; a program needn't handle non-finite values. No bound on the sum of `substance_label` on one device may be relied on, other than what follows from the above.
Results may differ from the reference program's by a relative error of at most 0.0028.
Values may be sent and summed in bfloat16 or wider, within the bound.
A program may use at most 192 MiB of HBM per device.

```python
import math
import jax
import jax.numpy as jnp
from jax import lax

M = 768
NB = 6
ND = 16
SWEEPS = 4
OUTER = 2
LATTICE_EAST = 128
LATTICE_NORTH = 128
LATTICE_UPWARD = 32


def touch_ends(drawn, key, low, high):
    longest = drawn.shape.index(max(drawn.shape))
    spots = []
    for shift in (0, 1):
        where = [jax.random.randint(jax.random.fold_in(key, axis), (), 0, length) for axis, length in enumerate(drawn.shape)]
        where[longest] = (where[longest] + shift) % drawn.shape[longest]
        spots.append(tuple(where))
    return drawn.at[spots[0]].set(low).at[spots[1]].set(high)


def level_of(stream_key, extent, pieces, low, largest):
    def one(dim, shards_of):
        draws = jax.random.uniform(jax.random.fold_in(jax.random.fold_in(stream_key, 6), dim), (shards_of,), jnp.float32, low / len(pieces), largest / len(pieces))
        return jnp.repeat(jnp.exp(draws), extent[dim] // shards_of).reshape((-1,) + (1,) * (len(extent) - dim - 1))

    gain = one(*pieces[0])
    for cut in pieces[1:]:
        gain = gain * one(*cut)
    return gain


def scatter_about(stream_key, shape, scale, limit, cuts=(), kind=jnp.bfloat16):
    drawn = scale * jax.random.normal(stream_key, shape, jnp.float32)
    if cuts:
        drawn = drawn * level_of(stream_key, shape, cuts, -0.22, 0.18)
    return jnp.clip(drawn, -limit, limit).astype(kind)


def setup_inputs(seed: int = 0) -> dict:
    seeds = jax.random.split(jax.random.key(seed), 10)
    excess_phonon_enthalpy = scatter_about(seeds[0], (M, LATTICE_UPWARD, LATTICE_EAST, LATTICE_NORTH), 0.036, 0.21972656, ((0, 8), (1, 4)))
    thermal_offset = scatter_about(seeds[1], (LATTICE_EAST, LATTICE_NORTH, LATTICE_UPWARD), 1.0, 6.0, ((0, 4), (1, 8)), jnp.float32)
    state_specific_warmth_scaled = jnp.clip(jnp.exp(math.log(2.0) - 1.3862944 * jax.random.uniform(seeds[2], (M,), jnp.float32) ** level_of(seeds[2], (M,), ((0, 8),), -0.2, 0.2)), 0.5, 2.0)
    scattering_lifetimes = jnp.clip(jnp.exp(math.log(50.0) - 4.6051702 * jax.random.uniform(seeds[3], (M,), jnp.float32) ** level_of(seeds[3], (M,), ((0, 8),), -0.2, 0.2)), 0.5, 50.0)
    state_polarization_label = touch_ends(jax.random.randint(seeds[4], (M,), 0, NB), jax.random.fold_in(seeds[4], 1), 0, NB - 1).astype(jnp.int32)
    state_orientation_label = touch_ends(jax.random.randint(seeds[5], (M,), 0, ND), jax.random.fold_in(seeds[5], 1), 0, ND - 1).astype(jnp.int32)
    polarization_propagation_rate = jnp.clip(jnp.exp(jax.random.uniform(seeds[6], (NB,), jnp.float32, math.log(0.3), math.log(1.0))), 0.3, 1.0)
    thermal_conductance_bulk = jnp.clip(0.25 + 0.75 * jax.random.uniform(seeds[7], (LATTICE_EAST, LATTICE_NORTH, LATTICE_UPWARD), jnp.float32) ** level_of(seeds[7], (LATTICE_EAST, LATTICE_NORTH, LATTICE_UPWARD), ((0, 4), (1, 8)), -0.2, 0.2), 0.25, 1.0)
    substance_label = touch_ends((jax.random.randint(seeds[8], (LATTICE_EAST, LATTICE_NORTH, LATTICE_UPWARD), 0, 4) < 1).astype(jnp.int32), jax.random.fold_in(seeds[8], 1), 0, 1)
    return {"excess_phonon_enthalpy": excess_phonon_enthalpy, "thermal_offset": thermal_offset, "state_specific_warmth_scaled": state_specific_warmth_scaled, "scattering_lifetimes": scattering_lifetimes, "state_polarization_label": state_polarization_label, "state_orientation_label": state_orientation_label, "polarization_propagation_rate": polarization_propagation_rate, "thermal_conductance_bulk": thermal_conductance_bulk, "substance_label": substance_label}


time_step = 0.25
pore_factor = 0.1
kappa_top = 1.0

def mode_table(state_polarization_label, state_orientation_label, state_specific_warmth_scaled, scattering_lifetimes, polarization_propagation_rate):
    branches = jnp.arange(polarization_propagation_rate.shape[0], dtype=jnp.int32)
    onehot = (state_polarization_label[:, None] == branches[None, :]).astype(jnp.float32)
    speed = lax.optimization_barrier(jnp.sum(onehot * polarization_propagation_rate[None, :], axis=1))
    polar = state_orientation_label // 4
    azimuth = state_orientation_label % 4
    cosine = (2 * polar + 1).astype(jnp.float32) * 0.25 - 1.0
    sine = jnp.sqrt(1.0 - cosine * cosine)
    angle = (azimuth.astype(jnp.float32) + 0.5) * (math.pi / 2.0)
    velocity = (speed * sine * jnp.cos(angle), speed * sine * jnp.sin(angle), speed * cosine)
    rates = 1.0 / scattering_lifetimes
    capacity = state_specific_warmth_scaled / float(M)
    return (velocity, rates, capacity)

def upwind(padded, temp_slab, along_x, along_y, along_z, rates, capacity):

    def widen(values):
        return values[:, None, None, None]
    current = padded[:, 1:-1]
    z_before = padded[:, :-2]
    z_after = padded[:, 2:]
    x_padded = jnp.pad(current, ((0, 0), (0, 0), (1, 1), (0, 0)))
    y_padded = jnp.pad(current, ((0, 0), (0, 0), (0, 0), (1, 1)))

    def advect(speed, before, after):
        flow = widen(speed)
        return jnp.maximum(flow, 0.0) * (current - before) + jnp.minimum(flow, 0.0) * (after - current)
    total_advect = advect(along_x, x_padded[:, :, :-2], x_padded[:, :, 2:])
    total_advect = total_advect + advect(along_y, y_padded[:, :, :, :-2], y_padded[:, :, :, 2:])
    total_advect = total_advect + advect(along_z, z_before, z_after)
    updated = current - time_step * total_advect + time_step * widen(rates) * (widen(capacity) * temp_slab[None] - current)
    weights = jnp.stack([rates, along_x, along_y, along_z])
    moments = jnp.einsum('km,mzxy->kzxy', weights, updated, precision=lax.Precision.HIGHEST)
    return (updated, moments)

def harmonic(first, second):
    summed = first + second
    positive = summed > 0.0
    return jnp.where(positive, 2.0 * first * second / jnp.where(positive, summed, 1.0), 0.0)

def face_table(kappa_ext):
    center = kappa_ext[1:-1, 1:-1]
    z_padded = jnp.pad(center, ((0, 0), (0, 0), (1, 1)))
    return (harmonic(center, kappa_ext[2:, 1:-1]), harmonic(kappa_ext[:-2, 1:-1], center), harmonic(center, kappa_ext[1:-1, 2:]), harmonic(kappa_ext[1:-1, :-2], center), harmonic(center, z_padded[:, :, 2:]), harmonic(z_padded[:, :, :-2], center))

def crop(values, matrix_height, matrix_breadth):
    top = (values.shape[0] - matrix_height) // 2
    left = (values.shape[1] - matrix_breadth) // 2
    return values[top:top + matrix_height, left:left + matrix_breadth]

def apply_operator(padded, faces, total):
    matrix_height = padded.shape[0] - 2
    matrix_breadth = padded.shape[1] - 2
    cut = [crop(face, matrix_height, matrix_breadth) for face in faces]
    center = padded[1:-1, 1:-1]
    z_padded = jnp.pad(center, ((0, 0), (0, 0), (1, 1)))
    spread = cut[0] * (padded[2:, 1:-1] - center) + cut[1] * (padded[:-2, 1:-1] - center)
    spread = spread + cut[2] * (padded[1:-1, 2:] - center) + cut[3] * (padded[1:-1, :-2] - center)
    spread = spread + cut[4] * (z_padded[:, :, 2:] - center) + cut[5] * (z_padded[:, :, :-2] - center)
    return total * center - spread

def divergence(fluxes):
    z_flux = jnp.pad(fluxes[2][1:-1, 1:-1], ((0, 0), (0, 0), (1, 1)))
    summed = fluxes[0][2:, 1:-1] - fluxes[0][:-2, 1:-1] + (fluxes[1][1:-1, 2:] - fluxes[1][1:-1, :-2])
    summed = summed + (z_flux[:, :, 2:] - z_flux[:, :, :-2])
    return summed * 0.5

def chebyshev(rhs, faces, total, extend, matrix_height, matrix_breadth):
    theta = total + 6.0 * kappa_top
    spread = 6.0 * kappa_top
    sigma = theta / spread
    rho = 1.0 / sigma
    residual = rhs
    direction = rhs / theta
    correction = jnp.zeros((matrix_height, matrix_breadth, rhs.shape[2]), jnp.float32)
    for sweep in range(SWEEPS):
        correction = correction + crop(direction, matrix_height, matrix_breadth)
        if sweep < SWEEPS - 1:
            image = apply_operator(extend(direction), faces, total)
            residual = crop(residual, image.shape[0], image.shape[1]) - image
            rho_next = 1.0 / (2.0 * sigma - rho)
            direction = rho_next * rho * crop(direction, image.shape[0], image.shape[1]) + 2.0 * rho_next / spread * residual
            rho = rho_next
    return correction

def pad_cycle(values):
    return jnp.pad(values, ((1, 1), (1, 1), (0, 0)))

def reference(excess_phonon_enthalpy, thermal_offset, state_specific_warmth_scaled, scattering_lifetimes, state_polarization_label, state_orientation_label, polarization_propagation_rate, thermal_conductance_bulk, substance_label):
    velocity, rates, capacity = mode_table(state_polarization_label, state_orientation_label, state_specific_warmth_scaled, scattering_lifetimes, polarization_propagation_rate)
    total = jnp.sum(capacity * rates)
    kappa = thermal_conductance_bulk * jnp.where(substance_label == 1, pore_factor, 1.0)
    faces = face_table(pad_cycle(kappa))
    spatial_entries = thermal_offset
    state = excess_phonon_enthalpy
    group = 16
    fluxes = None
    for outer in range(OUTER):
        temp_slab = jnp.transpose(spatial_entries, (2, 0, 1))
        shaped = state.reshape(M // group, group, LATTICE_UPWARD, LATTICE_EAST, LATTICE_NORTH)
        params = (velocity[0].reshape(-1, group), velocity[1].reshape(-1, group), velocity[2].reshape(-1, group), rates.reshape(-1, group), capacity.reshape(-1, group))

        def step(carry, inputs):
            block, along_x, along_y, along_z, rate_part, cap_part = inputs
            padded = jnp.pad(block.astype(jnp.float32), ((0, 0), (1, 1), (0, 0), (0, 0)))
            updated, moments = upwind(padded, temp_slab, along_x, along_y, along_z, rate_part, cap_part)
            return (carry + moments, updated.astype(jnp.bfloat16))
        start = jnp.zeros((4, LATTICE_UPWARD, LATTICE_EAST, LATTICE_NORTH), jnp.float32)
        moments, news = lax.scan(step, start, (shaped,) + params)
        state = news.reshape(M, LATTICE_UPWARD, LATTICE_EAST, LATTICE_NORTH)
        blocks = jnp.transpose(moments, (0, 2, 3, 1))
        fluxes = blocks[1:]
        rhs = -divergence(jnp.pad(fluxes, ((0, 0), (1, 1), (1, 1), (0, 0))))
        correction = chebyshev(rhs, faces, total, pad_cycle, LATTICE_EAST, LATTICE_NORTH)
        spatial_entries = blocks[0] / total + correction
    return (spatial_entries, fluxes)
```

```python
import functools
import math

import jax
import jax.numpy as jnp
from jax import lax
from jax.experimental import pallas as pl
from jax.experimental.pallas import tpu as pltpu
from jax.sharding import PartitionSpec as P

SWEEPS = 4
HALO = 2 * SWEEPS
time_step = 0.25
pore_factor = 0.1
kappa_top = 1.0

UNIT = ((1, 0, 0), (-1, 0, 0), (0, 1, 0), (0, -1, 0), (0, 0, 1), (0, 0, -1))
ONE = ((0, 0, 0),) + UNIT
PAIRS = tuple(
    (i, j)
    for i in range(6)
    for j in range(i, 6)
    if i // 2 != j // 2 or i == j
)
TWO = tuple(tuple(UNIT[i][a] + UNIT[j][a] for a in range(3)) for i, j in PAIRS)
OFFSETS = ONE + TWO


def mode_table(labels, orientation, warmth, lifetimes, rate_of, modes):
    branches = jnp.arange(rate_of.shape[0], dtype=jnp.int32)
    onehot = (labels[:, None] == branches[None, :]).astype(jnp.float32)
    speed = jnp.sum(onehot * rate_of[None, :], axis=1)
    polar = orientation // 4
    azimuth = orientation % 4
    cosine = (2 * polar + 1).astype(jnp.float32) * 0.25 - 1.0
    sine = jnp.sqrt(1.0 - cosine * cosine)
    angle = (azimuth.astype(jnp.float32) + 0.5) * (math.pi / 2.0)
    velocity = (speed * sine * jnp.cos(angle), speed * sine * jnp.sin(angle), speed * cosine)
    return velocity, 1.0 / lifetimes, warmth / float(modes)


def stencils(velocity, rates):
    push = []
    for v in velocity:
        push.append(time_step * jnp.maximum(v, 0.0))
        push.append(time_step * jnp.maximum(-v, 0.0))
    center = 1.0 - sum(push) - time_step * rates
    once = [center] + push
    twice = [center * center] + [2.0 * center * p for p in push]
    for i, j in PAIRS:
        twice.append((1.0 if i == j else 2.0) * push[i] * push[j])
    return jnp.stack(once), jnp.stack(twice)


def moments_kernel(e_ref, a_ref, out_ref, mid, plus, minus):
    z = pl.program_id(0)
    xb = pl.program_id(1)
    width = e_ref.shape[2]
    lanes = e_ref.shape[3]
    planes = mid.shape[0]
    across = mid.shape[1] - 4

    @pl.when((z == 0) & (xb == 0))
    def _():
        def clear(p, _):
            for ref in (mid, plus, minus):
                ref[p] = jnp.zeros(ref.shape[1:], jnp.float32)
            return 0

        lax.fori_loop(0, planes, clear, 0)

    lane = lax.broadcasted_iota(jnp.int32, (8, lanes), 1)
    turned = jnp.transpose(e_ref[:, 0], (1, 0, 2))
    a = a_ref[...]
    for i in range(0, width, 2):
        pair = jnp.concatenate([turned[i], turned[i + 1]], axis=1)
        fields = jnp.dot(
            a, jnp.concatenate([pair, pair], axis=0), preferred_element_type=jnp.float32
        )
        for j in range(2):
            x = xb * width + (i + j)
            for n, (dx, dy, dz) in enumerate(OFFSETS):
                part = fields[8 * n : 8 * n + 8, lanes * j : lanes * (j + 1)]
                if dy == 2:
                    part = jnp.where(lane >= 2, pltpu.roll(part, 2, 1), 0.0)
                elif dy == -2:
                    part = jnp.where(lane < lanes - 2, pltpu.roll(part, lanes - 2, 1), 0.0)
                ref = {1: plus, -1: minus}.get(dy, mid)
                ref[z + (2 + dz), x + (2 + dx)] += part

    @pl.when((z == pl.num_programs(0) - 1) & (xb == pl.num_programs(1) - 1))
    def _():
        spot = lax.broadcasted_iota(jnp.int32, (across, lanes), 1)
        blocks = out_ref.shape[0]
        deep = out_ref.shape[3]

        def finish(p, _):
            for k in range(8):
                up = pltpu.roll(plus[p, pl.ds(2, across), k, :], 1, 1)
                down = pltpu.roll(minus[p, pl.ds(2, across), k, :], lanes - 1, 1)
                whole = mid[p, pl.ds(2, across), k, :]
                whole = whole + jnp.where(spot >= 1, up, 0.0)
                whole = whole + jnp.where(spot < lanes - 1, down, 0.0)
                upright = whole.T
                for b in range(blocks):
                    out_ref[b, k, p] = upright[b * deep : (b + 1) * deep]
            return 0

        lax.fori_loop(0, planes, finish, 0)


def local_moments(state, table, blocks):
    modes, nz, nx, ny = state.shape
    width = math.gcd(nx, 16)
    acc = pltpu.VMEM((nz + 4, nx + 4, 8, ny), jnp.float32)
    shape = (blocks, 8, nz + 4, ny // blocks, nx)
    return pl.pallas_call(
        moments_kernel,
        grid=(nz, nx // width),
        in_specs=[
            pl.BlockSpec((modes, 1, width, ny), lambda z, x: (0, z, x, 0)),
            pl.BlockSpec(table.shape, lambda z, x: (0, 0)),
        ],
        out_specs=pl.BlockSpec(shape, lambda z, x: (0, 0, 0, 0, 0)),
        out_shape=jax.ShapeDtypeStruct(shape, jnp.float32),
        scratch_shapes=[acc, acc, acc],
        compiler_params=pltpu.CompilerParams(
            dimension_semantics=("arbitrary", "arbitrary"), vmem_limit_bytes=60 * 1024 * 1024
        ),
        name="moments",
    )(state, table)


def heat_kernel(s_ref, m_ref, t_ref, k_ref, temp_ref, flux_ref):
    ny, nx = t_ref.shape[1:]

    def shift(v, axis, step):
        if axis == 0:
            zero = jnp.zeros((1,) + v.shape[1:], v.dtype)
            return jnp.concatenate([v[1:], zero] if step > 0 else [zero, v[:-1]], axis=0)
        size = v.shape[axis]
        return pltpu.roll(v, (size - 1) if step > 0 else 1, axis)

    kappa = k_ref[...]
    inside = kappa > 0.0
    start = t_ref[...]
    total = s_ref[0]

    def harmonic(first, second):
        summed = first + second
        positive = summed > 0.0
        return jnp.where(positive, 2.0 * first * second / jnp.where(positive, summed, 1.0), 0.0)

    ahead = [harmonic(kappa, shift(kappa, axis, 1)) for axis in (2, 1, 0)]

    def operator(v):
        spread = None
        for axis, face in zip((2, 1, 0), ahead):
            flow = face * (shift(v, axis, 1) - v)
            term = flow - shift(flow, axis, -1)
            spread = term if spread is None else spread + term
        return total * v - spread

    def solve(flux):
        rhs = None
        for axis, f in zip((2, 1, 0), flux):
            term = shift(f, axis, 1) - shift(f, axis, -1)
            rhs = term if rhs is None else rhs + term
        rhs = rhs * -0.5
        theta = total + 6.0 * kappa_top
        spread = 6.0 * kappa_top
        sigma = theta / spread
        rho = 1.0 / sigma
        residual = rhs
        direction = rhs / theta
        correction = direction
        for _ in range(SWEEPS - 1):
            residual = residual - operator(direction)
            rho_next = 1.0 / (2.0 * sigma - rho)
            direction = rho_next * rho * direction + 2.0 * rho_next / spread * residual
            rho = rho_next
            correction = correction + direction
        return correction

    first = [m_ref[k] + s_ref[1 + k] * start for k in range(4)]
    middle = jnp.where(inside, first[0] / total + solve(first[1:]), 0.0)
    moved = [start] + [shift(start, 2 - axis, -step) for axis in range(3) for step in (1, -1)]
    second = []
    for k in range(4):
        value = m_ref[4 + k] + s_ref[1 + k] * middle
        for n, m in enumerate(moved):
            value = value + s_ref[5 + 7 * k + n] * m
        second.append(jnp.where(inside, value, 0.0))
    temp_ref[...] = second[0] / total + solve(second[1:])
    for a in range(3):
        flux_ref[a] = second[1 + a]


def heat(scalars, moments, temp, kappa):
    shape = temp.shape
    return pl.pallas_call(
        heat_kernel,
        in_specs=[pl.BlockSpec(memory_space=pltpu.SMEM)]
        + [pl.BlockSpec(memory_space=pltpu.VMEM)] * 3,
        out_specs=[pl.BlockSpec(memory_space=pltpu.VMEM)] * 2,
        out_shape=[
            jax.ShapeDtypeStruct(shape, jnp.float32),
            jax.ShapeDtypeStruct((3,) + shape, jnp.float32),
        ],
        compiler_params=pltpu.CompilerParams(vmem_limit_bytes=60 * 1024 * 1024),
        name="heat",
    )(scalars, moments, temp, kappa)


def widen(cells, sides, width):
    for axis, dim in sides:
        count = lax.axis_size(axis)
        ends = count - 1
        head = lax.slice_in_dim(cells, 0, width, axis=dim)
        tail = lax.slice_in_dim(cells, cells.shape[dim] - width, cells.shape[dim], axis=dim)
        cells = jnp.concatenate(
            [
                lax.ppermute(tail, axis, [(i, i + 1) for i in range(ends)]),
                cells,
                lax.ppermute(head, axis, [(i + 1, i) for i in range(ends)]),
            ],
            axis=dim,
        )
    return cells


def per_device(
    excess_phonon_enthalpy,
    thermal_offset,
    state_specific_warmth_scaled,
    scattering_lifetimes,
    state_polarization_label,
    state_orientation_label,
    polarization_propagation_rate,
    thermal_conductance_bulk,
    substance_label,
):
    groups = lax.axis_size("mode")
    slabs = lax.axis_size("space")
    modes = state_orientation_label.shape[0]
    velocity, rates, capacity = mode_table(
        state_polarization_label,
        state_orientation_label,
        state_specific_warmth_scaled,
        scattering_lifetimes,
        polarization_propagation_rate,
        modes * groups,
    )
    once, twice = stencils(velocity, rates)
    weights = jnp.stack([rates, *velocity])
    gain = time_step * rates * capacity
    sums = jnp.concatenate(
        [
            jnp.sum(capacity * rates)[None],
            jnp.sum(weights * gain, axis=1),
            jnp.sum((weights * gain)[:, None, :] * once[None], axis=2).reshape(-1),
        ]
    )
    scalars = lax.psum(sums, "mode")

    lone = jnp.zeros((len(TWO), modes), jnp.float32)
    table = jnp.stack([jnp.concatenate([once, lone]), twice], axis=1)
    table = (table[:, :, None, :] * weights[None, None]).reshape(8 * len(OFFSETS), modes)
    high = table.astype(jnp.bfloat16)
    low = (table - high.astype(jnp.float32)).astype(jnp.bfloat16)
    table = jnp.concatenate([high, low], axis=1)

    kappa = thermal_conductance_bulk * jnp.where(substance_label == 1, pore_factor, 1.0)
    sides = (("space", 3), ("mode", 2))
    start = jnp.transpose(jnp.stack([thermal_offset, kappa]), (0, 3, 2, 1))
    start = widen(start, sides, HALO)

    partial = local_moments(excess_phonon_enthalpy, table, groups)
    reduced = lax.psum_scatter(partial, "mode", scatter_dimension=0, tiled=True)[0]
    _, deep, ny, nx = reduced.shape
    nz = deep - 4
    part = nx // slabs
    cut = reduced.reshape(8, deep, ny, slabs, part)
    cut = jnp.transpose(cut, (3, 0, 1, 2, 4))
    cut = lax.all_to_all(cut, "space", split_axis=0, concat_axis=0, tiled=True)
    height = nz * slabs
    summed = None
    for s in range(slabs):
        term = jnp.pad(cut[s], ((0, 0), (s * nz, height - (s + 1) * nz), (0, 0), (0, 0)))
        summed = term if summed is None else summed + term
    summed = summed[:, 2:-2]
    moments = widen(summed, sides, HALO)

    def fill(values):
        extra = -values.shape[-1] % 128
        return jnp.pad(values, ((0, 0),) * (values.ndim - 1) + ((0, extra),))

    temp, flux = heat(scalars, fill(moments), fill(start[0]), fill(start[1]))
    rows = slice(HALO, HALO + ny)
    columns = slice(HALO, HALO + part)
    return (
        jnp.transpose(temp[:, rows, columns], (2, 1, 0)),
        jnp.transpose(flux[:, :, rows, columns], (0, 3, 2, 1)),
    )


def solution(mesh):
    placed = (
        P("mode", "space", None, None),
        P("space", "mode", None),
        P("mode"),
        P("mode"),
        P("mode"),
        P("mode"),
        P(),
        P("space", "mode", None),
        P("space", "mode", None),
    )
    return jax.shard_map(
        per_device,
        mesh=mesh,
        in_specs=placed,
        out_specs=(P("space", "mode", None), P(None, "space", "mode", None)),
        check_vma=False,
    )
```

```python
import functools
import math

import jax
import jax.numpy as jnp
from jax import lax
from jax.experimental import pallas as pl
from jax.experimental.pallas import tpu as pltpu
from jax.sharding import PartitionSpec as P

SWEEPS = 4
HALO = 2 * SWEEPS
time_step = 0.25
pore_factor = 0.1
kappa_top = 1.0

UNIT = ((1, 0, 0), (-1, 0, 0), (0, 1, 0), (0, -1, 0), (0, 0, 1), (0, 0, -1))
ONE = ((0, 0, 0),) + UNIT
PAIRS = tuple(
    (i, j)
    for i in range(6)
    for j in range(i, 6)
    if i // 2 != j // 2 or i == j
)
TWO = tuple(tuple(UNIT[i][a] + UNIT[j][a] for a in range(3)) for i, j in PAIRS)
OFFSETS = ONE + TWO


def mode_table(labels, orientation, warmth, lifetimes, rate_of, modes):
    branches = jnp.arange(rate_of.shape[0], dtype=jnp.int32)
    onehot = (labels[:, None] == branches[None, :]).astype(jnp.float32)
    speed = jnp.sum(onehot * rate_of[None, :], axis=1)
    polar = orientation // 4
    azimuth = orientation % 4
    cosine = (2 * polar + 1).astype(jnp.float32) * 0.25 - 1.0
    sine = jnp.sqrt(1.0 - cosine * cosine)
    angle = (azimuth.astype(jnp.float32) + 0.5) * (math.pi / 2.0)
    velocity = (speed * sine * jnp.cos(angle), speed * sine * jnp.sin(angle), speed * cosine)
    return velocity, 1.0 / lifetimes, warmth / float(modes)


def stencils(velocity, rates):
    push = []
    for v in velocity:
        push.append(time_step * jnp.maximum(v, 0.0))
        push.append(time_step * jnp.maximum(-v, 0.0))
    center = 1.0 - sum(push) - time_step * rates
    once = [center] + push
    twice = [center * center] + [2.0 * center * p for p in push]
    for i, j in PAIRS:
        twice.append((1.0 if i == j else 2.0) * push[i] * push[j])
    return jnp.stack(once), jnp.stack(twice)


def moments_kernel(place_ref, e_ref, a_ref, sums_ref, out_ref, mid, plus, minus):
    z = pl.program_id(0)
    xb = pl.program_id(1)
    width = e_ref.shape[2]
    lanes = e_ref.shape[3]
    planes = mid.shape[0]
    across = mid.shape[1] - 4

    @pl.when((z == 0) & (xb == 0))
    def _():
        def clear(p, _):
            for ref in (mid, plus, minus):
                ref[p] = jnp.zeros(ref.shape[1:], jnp.float32)
            return 0

        lax.fori_loop(0, planes, clear, 0)

    lane = lax.broadcasted_iota(jnp.int32, (8, lanes), 1)
    turned = jnp.transpose(e_ref[:, 0], (1, 0, 2))
    a = a_ref[...]
    for i in range(0, width, 2):
        pair = jnp.concatenate([turned[i], turned[i + 1]], axis=1)
        fields = jnp.dot(
            a, jnp.concatenate([pair, pair], axis=0), preferred_element_type=jnp.float32
        )
        for j in range(2):
            x = xb * width + (i + j)
            for n, (dx, dy, dz) in enumerate(OFFSETS):
                part = fields[8 * n : 8 * n + 8, lanes * j : lanes * (j + 1)]
                if dy == 2:
                    part = jnp.where(lane >= 2, pltpu.roll(part, 2, 1), 0.0)
                elif dy == -2:
                    part = jnp.where(lane < lanes - 2, pltpu.roll(part, lanes - 2, 1), 0.0)
                ref = {1: plus, -1: minus}.get(dy, mid)
                ref[z + (2 + dz), x + (2 + dx)] += part

    @pl.when((z == pl.num_programs(0) - 1) & (xb == pl.num_programs(1) - 1))
    def _():
        spot = lax.broadcasted_iota(jnp.int32, (across, lanes), 1)
        blocks = out_ref.shape[0]
        deep = out_ref.shape[3]

        row = lax.broadcasted_iota(jnp.int32, (lanes, across), 0)
        column = lax.broadcasted_iota(jnp.int32, (lanes, across), 1)

        def put(k, p, value):
            for b in range(blocks):
                out_ref[b, k, p] = value[b * deep : (b + 1) * deep]

        def difference(value, axis):
            spots = (row, column)[axis]
            size = value.shape[axis]
            after = jnp.where(spots < size - 1, pltpu.roll(value, size - 1, axis), 0.0)
            return after - jnp.where(spots >= 1, pltpu.roll(value, 1, axis), 0.0)

        def finish(p, below):
            upright = []
            for k in range(8):
                up = pltpu.roll(plus[p, pl.ds(2, across), k, :], 1, 1)
                down = pltpu.roll(minus[p, pl.ds(2, across), k, :], lanes - 1, 1)
                whole = mid[p, pl.ds(2, across), k, :]
                whole = whole + jnp.where(spot >= 1, up, 0.0)
                whole = whole + jnp.where(spot < lanes - 1, down, 0.0)
                upright.append(whole.T)
            put(0, p, upright[0])
            inside = (p >= place_ref[0]) & (p < place_ref[1])
            flux = [jnp.where(inside, v, 0.0) for v in upright[1:4]]
            put(1, p, difference(flux[0], 1) + difference(flux[1], 0) - below)
            under = jnp.maximum(p - 1, 0)
            for b in range(blocks):
                out_ref[b, 1, under] += flux[2][b * deep : (b + 1) * deep]
            for k in range(4):
                put(2 + k, p, upright[4 + k])
            return flux[2]

        lax.fori_loop(0, planes, finish, jnp.zeros((lanes, across), jnp.float32))
        for b in range(blocks):
            out_ref[b, 0, 0] = jnp.broadcast_to(sums_ref[...], (deep, across))


def local_moments(place, state, table, sums, blocks):
    modes, nz, nx, ny = state.shape
    width = math.gcd(nx, 16)
    acc = pltpu.VMEM((nz + 4, nx + 4, 8, ny), jnp.float32)
    shape = (blocks, 6, nz + 4, ny // blocks, nx)
    return pl.pallas_call(
        moments_kernel,
        grid=(nz, nx // width),
        in_specs=[
            pl.BlockSpec(memory_space=pltpu.SMEM),
            pl.BlockSpec((modes, 1, width, ny), lambda z, x: (0, z, x, 0)),
            pl.BlockSpec(table.shape, lambda z, x: (0, 0)),
            pl.BlockSpec(sums.shape, lambda z, x: (0, 0)),
        ],
        out_specs=pl.BlockSpec(shape, lambda z, x: (0, 0, 0, 0, 0)),
        out_shape=jax.ShapeDtypeStruct(shape, jnp.float32),
        scratch_shapes=[acc, acc, acc],
        compiler_params=pltpu.CompilerParams(
            dimension_semantics=("arbitrary", "arbitrary"), vmem_limit_bytes=60 * 1024 * 1024
        ),
        name="moments",
    )(place, state, table, sums)


def heat_kernel(s_ref, m_ref, low_ref, high_ref, t_ref, k_ref, temp_ref, flux_ref):
    lane = lax.broadcasted_iota(jnp.int32, t_ref.shape, 2)

    def shift(v, axis, step):
        if axis == 0:
            zero = jnp.zeros((1,) + v.shape[1:], v.dtype)
            return jnp.concatenate([v[1:], zero] if step > 0 else [zero, v[:-1]], axis=0)
        size = v.shape[axis]
        moved = pltpu.roll(v, (size - 1) if step > 0 else 1, axis)
        if axis == 2:
            moved = jnp.where(lane < size - 1 if step > 0 else lane >= 1, moved, 0.0)
        return moved

    def field(k):
        return jnp.concatenate([low_ref[k], m_ref[k], high_ref[k]], axis=1)

    kappa = k_ref[...]
    inside = kappa > 0.0
    start = t_ref[...]
    total = s_ref[0]

    def harmonic(first, second):
        summed = first + second
        positive = summed > 0.0
        return jnp.where(positive, 2.0 * first * second / jnp.where(positive, summed, 1.0), 0.0)

    ahead = [harmonic(kappa, shift(kappa, axis, 1)) for axis in (2, 1, 0)]

    def operator(v):
        spread = None
        for axis, face in zip((2, 1, 0), ahead):
            flow = face * (shift(v, axis, 1) - v)
            term = flow - shift(flow, axis, -1)
            spread = term if spread is None else spread + term
        return total * v - spread

    def solve(flux, rhs=0.0):
        for axis, f in zip((2, 1, 0), flux):
            rhs = rhs + (shift(f, axis, 1) - shift(f, axis, -1))
        rhs = rhs * -0.5
        theta = total + 6.0 * kappa_top
        spread = 6.0 * kappa_top
        sigma = theta / spread
        rho = 1.0 / sigma
        residual = rhs
        direction = rhs / theta
        correction = direction
        for _ in range(SWEEPS - 1):
            residual = residual - operator(direction)
            rho_next = 1.0 / (2.0 * sigma - rho)
            direction = rho_next * rho * direction + 2.0 * rho_next / spread * residual
            rho = rho_next
            correction = correction + direction
        return correction

    weight = field(0) + s_ref[1] * start
    change = solve([s_ref[2 + a] * start for a in range(3)], field(1))
    middle = jnp.where(inside, weight / total + change, 0.0)
    moved = [start] + [shift(start, 2 - axis, -step) for axis in range(3) for step in (1, -1)]
    second = []
    for k in range(4):
        value = field(2 + k) + s_ref[1 + k] * middle
        for n, m in enumerate(moved):
            value = value + s_ref[5 + 7 * k + n] * m
        second.append(jnp.where(inside, value, 0.0))
    rows = slice(HALO, t_ref.shape[1] - HALO)
    temp_ref[...] = (second[0] / total + solve(second[1:]))[:, rows]
    for a in range(3):
        flux_ref[a] = second[1 + a][:, rows]


def heat(scalars, moments, low, high, temp, kappa):
    shape = moments.shape[1:]
    return pl.pallas_call(
        heat_kernel,
        in_specs=[pl.BlockSpec(memory_space=pltpu.SMEM)]
        + [pl.BlockSpec(memory_space=pltpu.VMEM)] * 5,
        out_specs=[pl.BlockSpec(memory_space=pltpu.VMEM)] * 2,
        out_shape=[
            jax.ShapeDtypeStruct(shape, jnp.float32),
            jax.ShapeDtypeStruct((3,) + shape, jnp.float32),
        ],
        compiler_params=pltpu.CompilerParams(vmem_limit_bytes=60 * 1024 * 1024),
        name="heat",
    )(scalars, moments, low, high, temp, kappa)


def beside(cells, dim, width):
    ends = lax.axis_size("mode") - 1
    head = lax.slice_in_dim(cells, 0, width, axis=dim)
    tail = lax.slice_in_dim(cells, cells.shape[dim] - width, cells.shape[dim], axis=dim)
    return (
        lax.ppermute(tail, "mode", [(i, i + 1) for i in range(ends)]),
        lax.ppermute(head, "mode", [(i + 1, i) for i in range(ends)]),
    )


def per_device(
    excess_phonon_enthalpy,
    thermal_offset,
    state_specific_warmth_scaled,
    scattering_lifetimes,
    state_polarization_label,
    state_orientation_label,
    polarization_propagation_rate,
    thermal_conductance_bulk,
    substance_label,
):
    groups = lax.axis_size("mode")
    slabs = lax.axis_size("space")
    modes = state_orientation_label.shape[0]
    velocity, rates, capacity = mode_table(
        state_polarization_label,
        state_orientation_label,
        state_specific_warmth_scaled,
        scattering_lifetimes,
        polarization_propagation_rate,
        modes * groups,
    )
    once, twice = stencils(velocity, rates)
    weights = jnp.stack([rates, *velocity])
    gain = time_step * rates * capacity
    sums = jnp.concatenate(
        [
            jnp.sum(capacity * rates)[None],
            jnp.sum(weights * gain, axis=1),
            jnp.sum((weights * gain)[:, None, :] * once[None], axis=2).reshape(-1),
        ]
    )

    lone = jnp.zeros((len(TWO), modes), jnp.float32)
    table = jnp.stack([jnp.concatenate([once, lone]), twice], axis=1)
    table = (table[:, :, None, :] * weights[None, None]).reshape(8 * len(OFFSETS), modes)
    high = lax.reduce_precision(table, 8, 7)
    table = jnp.concatenate([high, table - high], axis=1).astype(jnp.bfloat16)

    kappa = thermal_conductance_bulk * jnp.where(substance_label == 1, pore_factor, 1.0)
    start = jnp.transpose(jnp.stack([thermal_offset, kappa]), (0, 3, 1, 2))
    start = jnp.transpose(lax.all_gather(start, "space", axis=2, tiled=True), (0, 1, 3, 2))
    low, high = beside(start, 2, HALO)
    start = jnp.concatenate([low, start, high], axis=2)

    nz, nx, ny = excess_phonon_enthalpy.shape[1:]
    spot = lax.axis_index("space")
    place = jnp.stack([jnp.where(spot == 0, 2, 0), jnp.where(spot == slabs - 1, nz + 2, nz + 4)])
    sums = jnp.pad(sums, (0, nx - sums.shape[0]))[None]
    partial = local_moments(place.astype(jnp.int32), excess_phonon_enthalpy, table, sums, groups)
    reduced = lax.psum_scatter(partial, "mode", scatter_dimension=0, tiled=True)[0]
    scalars = reduced[0, 0, 0]
    slab = lax.all_gather(reduced, "space", axis=0)
    height = nz * slabs
    summed = None
    for s in range(slabs):
        term = slab[s]
        term = jnp.concatenate([jnp.zeros_like(term[:1, :1]), term[:1, 1:]], axis=1)
        term = jnp.concatenate([term, slab[s, 1:]], axis=0)
        term = jnp.pad(term, ((0, 0), (s * nz, height - (s + 1) * nz), (0, 0), (0, 0)))
        summed = term if summed is None else summed + term
    summed = summed[:, 2:-2]
    low, high = beside(summed, 2, HALO)
    temp, flux = heat(scalars, summed, low, high, start[0], start[1])
    part = nx // slabs
    temp = lax.dynamic_slice_in_dim(temp, spot * part, part, axis=2)
    flux = lax.dynamic_slice_in_dim(flux, spot * part, part, axis=3)
    return jnp.transpose(temp, (2, 1, 0)), jnp.transpose(flux, (0, 3, 2, 1))


def solution(mesh):
    placed = (
        P("mode", "space", None, None),
        P("space", "mode", None),
        P("mode"),
        P("mode"),
        P("mode"),
        P("mode"),
        P(),
        P("space", "mode", None),
        P("space", "mode", None),
    )
    return jax.shard_map(
        per_device,
        mesh=mesh,
        in_specs=placed,
        out_specs=(P("space", "mode", None), P(None, "space", "mode", None)),
        check_vma=False,
    )
```

```python
import functools
import math

import jax
import jax.numpy as jnp
from jax import lax
from jax.experimental import pallas as pl
from jax.experimental.pallas import tpu as pltpu
from jax.sharding import PartitionSpec as P

SWEEPS = 4
HALO = 2 * SWEEPS
time_step = 0.25
pore_factor = 0.1
kappa_top = 1.0

UNIT = ((1, 0, 0), (-1, 0, 0), (0, 1, 0), (0, -1, 0), (0, 0, 1), (0, 0, -1))
ONE = ((0, 0, 0),) + UNIT
PAIRS = tuple(
    (i, j)
    for i in range(6)
    for j in range(i, 6)
    if i // 2 != j // 2 or i == j
)
TWO = tuple(tuple(UNIT[i][a] + UNIT[j][a] for a in range(3)) for i, j in PAIRS)
OFFSETS = ONE + TWO


def mode_table(labels, orientation, warmth, lifetimes, rate_of, modes):
    branches = jnp.arange(rate_of.shape[0], dtype=jnp.int32)
    onehot = (labels[:, None] == branches[None, :]).astype(jnp.float32)
    speed = jnp.sum(onehot * rate_of[None, :], axis=1)
    polar = orientation // 4
    azimuth = orientation % 4
    cosine = (2 * polar + 1).astype(jnp.float32) * 0.25 - 1.0
    sine = jnp.sqrt(1.0 - cosine * cosine)
    angle = (azimuth.astype(jnp.float32) + 0.5) * (math.pi / 2.0)
    velocity = (speed * sine * jnp.cos(angle), speed * sine * jnp.sin(angle), speed * cosine)
    return velocity, 1.0 / lifetimes, warmth / float(modes)


def stencils(velocity, rates):
    push = []
    for v in velocity:
        push.append(time_step * jnp.maximum(v, 0.0))
        push.append(time_step * jnp.maximum(-v, 0.0))
    center = 1.0 - sum(push) - time_step * rates
    once = [center] + push
    twice = [center * center] + [2.0 * center * p for p in push]
    for i, j in PAIRS:
        twice.append((1.0 if i == j else 2.0) * push[i] * push[j])
    return jnp.stack(once), jnp.stack(twice)


def moments_kernel(place_ref, e_ref, a_ref, sums_ref, out_ref, mid, plus, minus):
    z = pl.program_id(0)
    xb = pl.program_id(1)
    width = e_ref.shape[2]
    lanes = e_ref.shape[3]
    planes = mid.shape[0]
    across = mid.shape[1] // 8 - 4

    @pl.when((z == 0) & (xb == 0))
    def _():
        def clear(p, _):
            for ref in (mid, plus, minus):
                ref[p] = jnp.zeros(ref.shape[1:], jnp.float32)
            return 0

        lax.fori_loop(0, planes, clear, 0)

    lane = lax.broadcasted_iota(jnp.int32, (8, lanes), 1)
    turned = jnp.transpose(e_ref[:, 0], (1, 0, 2))
    a = a_ref[...]
    for i in range(0, width, 2):
        pair = jnp.concatenate([turned[i], turned[i + 1]], axis=1)
        fields = jnp.dot(
            a, jnp.concatenate([pair, pair], axis=0), preferred_element_type=jnp.float32
        )
        for j in range(2):
            x = xb * width + (i + j)
            for n, (dx, dy, dz) in enumerate(OFFSETS):
                part = fields[8 * n : 8 * n + 8, lanes * j : lanes * (j + 1)]
                if dy == 2:
                    part = jnp.where(lane >= 2, pltpu.roll(part, 2, 1), 0.0)
                elif dy == -2:
                    part = jnp.where(lane < lanes - 2, pltpu.roll(part, lanes - 2, 1), 0.0)
                ref = {1: plus, -1: minus}.get(dy, mid)
                ref[z + (2 + dz), pl.ds(pl.multiple_of(8 * (x + (2 + dx)), 8), 8), :] += part

    @pl.when((z == pl.num_programs(0) - 1) & (xb == pl.num_programs(1) - 1))
    def _():
        spot = lax.broadcasted_iota(jnp.int32, (across, lanes), 1)
        blocks = out_ref.shape[0]
        deep = out_ref.shape[3]

        row = lax.broadcasted_iota(jnp.int32, (lanes, across), 0)
        column = lax.broadcasted_iota(jnp.int32, (lanes, across), 1)

        def put(k, p, value):
            for b in range(blocks):
                out_ref[b, k, p] = value[b * deep : (b + 1) * deep]

        def difference(value, axis):
            spots = (row, column)[axis]
            size = value.shape[axis]
            after = jnp.where(spots < size - 1, pltpu.roll(value, size - 1, axis), 0.0)
            return after - jnp.where(spots >= 1, pltpu.roll(value, 1, axis), 0.0)

        def finish(p, below):
            upright = []
            for k in range(8):
                up = pltpu.roll(plus[p, pl.ds(16 + k, across, stride=8), :], 1, 1)
                down = pltpu.roll(minus[p, pl.ds(16 + k, across, stride=8), :], lanes - 1, 1)
                whole = mid[p, pl.ds(16 + k, across, stride=8), :]
                whole = whole + jnp.where(spot >= 1, up, 0.0)
                whole = whole + jnp.where(spot < lanes - 1, down, 0.0)
                upright.append(whole.T)
            put(0, p, upright[0])
            inside = (p >= place_ref[0]) & (p < place_ref[1])
            flux = [jnp.where(inside, v, 0.0) for v in upright[1:4]]
            put(1, p, difference(flux[0], 1) + difference(flux[1], 0) - below)
            under = jnp.maximum(p - 1, 0)
            for b in range(blocks):
                out_ref[b, 1, under] += flux[2][b * deep : (b + 1) * deep]
            for k in range(4):
                put(2 + k, p, upright[4 + k])
            return flux[2]

        lax.fori_loop(0, planes, finish, jnp.zeros((lanes, across), jnp.float32))
        for b in range(blocks):
            out_ref[b, 0, 0] = jnp.broadcast_to(sums_ref[...], (deep, across))


def local_moments(place, state, table, sums, blocks):
    modes, nz, nx, ny = state.shape
    width = math.gcd(nx, 16)
    acc = pltpu.VMEM((nz + 4, 8 * (nx + 4), ny), jnp.float32)
    shape = (blocks, 6, nz + 4, ny // blocks, nx)
    return pl.pallas_call(
        moments_kernel,
        grid=(nz, nx // width),
        in_specs=[
            pl.BlockSpec(memory_space=pltpu.SMEM),
            pl.BlockSpec((modes, 1, width, ny), lambda z, x: (0, z, x, 0)),
            pl.BlockSpec(table.shape, lambda z, x: (0, 0)),
            pl.BlockSpec(sums.shape, lambda z, x: (0, 0)),
        ],
        out_specs=pl.BlockSpec(shape, lambda z, x: (0, 0, 0, 0, 0)),
        out_shape=jax.ShapeDtypeStruct(shape, jnp.float32),
        scratch_shapes=[acc, acc, acc],
        cost_estimate=pl.CostEstimate(
            flops=2 * table.shape[0] * table.shape[1] * nz * nx * ny,
            bytes_accessed=2 * state.size,
            transcendentals=0,
        ),
        compiler_params=pltpu.CompilerParams(
            dimension_semantics=("arbitrary", "arbitrary"), vmem_limit_bytes=60 * 1024 * 1024
        ),
        name="moments",
    )(place, state, table, sums)


def heat_kernel(s_ref, m_ref, low_ref, high_ref, t_ref, k_ref, temp_ref, flux_ref):
    lane = lax.broadcasted_iota(jnp.int32, t_ref.shape, 2)

    def shift(v, axis, step):
        if axis == 0:
            zero = jnp.zeros((1,) + v.shape[1:], v.dtype)
            return jnp.concatenate([v[1:], zero] if step > 0 else [zero, v[:-1]], axis=0)
        size = v.shape[axis]
        moved = pltpu.roll(v, (size - 1) if step > 0 else 1, axis)
        if axis == 2:
            moved = jnp.where(lane < size - 1 if step > 0 else lane >= 1, moved, 0.0)
        return moved

    def field(k):
        return jnp.concatenate([low_ref[k], m_ref[k], high_ref[k]], axis=1)

    kappa = k_ref[...]
    inside = kappa > 0.0
    start = t_ref[...]
    total = s_ref[0]

    def harmonic(first, second):
        summed = first + second
        positive = summed > 0.0
        return jnp.where(positive, 2.0 * first * second / jnp.where(positive, summed, 1.0), 0.0)

    ahead = [harmonic(kappa, shift(kappa, axis, 1)) for axis in (2, 1, 0)]

    def operator(v):
        spread = None
        for axis, face in zip((2, 1, 0), ahead):
            flow = face * (shift(v, axis, 1) - v)
            term = flow - shift(flow, axis, -1)
            spread = term if spread is None else spread + term
        return total * v - spread

    def solve(flux, rhs=0.0):
        for axis, f in zip((2, 1, 0), flux):
            rhs = rhs + (shift(f, axis, 1) - shift(f, axis, -1))
        rhs = rhs * -0.5
        theta = total + 6.0 * kappa_top
        spread = 6.0 * kappa_top
        sigma = theta / spread
        rho = 1.0 / sigma
        residual = rhs
        direction = rhs / theta
        correction = direction
        for _ in range(SWEEPS - 1):
            residual = residual - operator(direction)
            rho_next = 1.0 / (2.0 * sigma - rho)
            direction = rho_next * rho * direction + 2.0 * rho_next / spread * residual
            rho = rho_next
            correction = correction + direction
        return correction

    weight = field(0) + s_ref[1] * start
    change = solve([s_ref[2 + a] * start for a in range(3)], field(1))
    middle = jnp.where(inside, weight / total + change, 0.0)
    moved = [start] + [shift(start, 2 - axis, -step) for axis in range(3) for step in (1, -1)]
    second = []
    for k in range(4):
        value = field(2 + k) + s_ref[1 + k] * middle
        for n, m in enumerate(moved):
            value = value + s_ref[5 + 7 * k + n] * m
        second.append(jnp.where(inside, value, 0.0))
    rows = slice(HALO, t_ref.shape[1] - HALO)
    temp_ref[...] = (second[0] / total + solve(second[1:]))[:, rows]
    for a in range(3):
        flux_ref[a] = second[1 + a][:, rows]


def heat(scalars, moments, low, high, temp, kappa):
    shape = moments.shape[1:]
    return pl.pallas_call(
        heat_kernel,
        in_specs=[pl.BlockSpec(memory_space=pltpu.SMEM)]
        + [pl.BlockSpec(memory_space=pltpu.VMEM)] * 5,
        out_specs=[pl.BlockSpec(memory_space=pltpu.VMEM)] * 2,
        out_shape=[
            jax.ShapeDtypeStruct(shape, jnp.float32),
            jax.ShapeDtypeStruct((3,) + shape, jnp.float32),
        ],
        compiler_params=pltpu.CompilerParams(vmem_limit_bytes=60 * 1024 * 1024),
        name="heat",
    )(scalars, moments, low, high, temp, kappa)


def beside(cells, dim, width):
    ends = lax.axis_size("mode") - 1
    head = lax.slice_in_dim(cells, 0, width, axis=dim)
    tail = lax.slice_in_dim(cells, cells.shape[dim] - width, cells.shape[dim], axis=dim)
    return (
        lax.ppermute(tail, "mode", [(i, i + 1) for i in range(ends)]),
        lax.ppermute(head, "mode", [(i + 1, i) for i in range(ends)]),
    )


def per_device(
    excess_phonon_enthalpy,
    thermal_offset,
    state_specific_warmth_scaled,
    scattering_lifetimes,
    state_polarization_label,
    state_orientation_label,
    polarization_propagation_rate,
    thermal_conductance_bulk,
    substance_label,
):
    groups = lax.axis_size("mode")
    slabs = lax.axis_size("space")
    modes = state_orientation_label.shape[0]
    velocity, rates, capacity = mode_table(
        state_polarization_label,
        state_orientation_label,
        state_specific_warmth_scaled,
        scattering_lifetimes,
        polarization_propagation_rate,
        modes * groups,
    )
    once, twice = stencils(velocity, rates)
    weights = jnp.stack([rates, *velocity])
    gain = time_step * rates * capacity
    sums = jnp.concatenate(
        [
            jnp.sum(capacity * rates)[None],
            jnp.sum(weights * gain, axis=1),
            jnp.sum((weights * gain)[:, None, :] * once[None], axis=2).reshape(-1),
        ]
    )

    lone = jnp.zeros((len(TWO), modes), jnp.float32)
    table = jnp.stack([jnp.concatenate([once, lone]), twice], axis=1)
    table = (table[:, :, None, :] * weights[None, None]).reshape(8 * len(OFFSETS), modes)
    high = lax.reduce_precision(table, 8, 7)
    table = jnp.concatenate([high, table - high], axis=1).astype(jnp.bfloat16)

    kappa = thermal_conductance_bulk * jnp.where(substance_label == 1, pore_factor, 1.0)
    start = jnp.transpose(jnp.stack([thermal_offset, kappa]), (0, 3, 2, 1))
    start = lax.all_gather(start, "space", axis=0)
    start = jnp.concatenate([start[s] for s in range(slabs)], axis=3)
    low, high = beside(start, 2, HALO)
    start = jnp.concatenate([low, start, high], axis=2)

    nz, nx, ny = excess_phonon_enthalpy.shape[1:]
    spot = lax.axis_index("space")
    place = jnp.stack([jnp.where(spot == 0, 2, 0), jnp.where(spot == slabs - 1, nz + 2, nz + 4)])
    sums = jnp.pad(sums, (0, nx - sums.shape[0]))[None]
    partial = local_moments(place.astype(jnp.int32), excess_phonon_enthalpy, table, sums, groups)
    reduced = lax.psum_scatter(partial, "mode", scatter_dimension=0, tiled=True)[0]
    reduced, start = lax.optimization_barrier((reduced, start))
    scalars, reduced = lax.optimization_barrier((reduced[0, 0, 0], reduced))
    reduced = reduced.at[0, 0].set(0.0)
    slab = lax.all_gather(reduced, "space", axis=0)
    height = nz * slabs
    summed = None
    for s in range(slabs):
        term = jnp.pad(slab[s], ((0, 0), (s * nz, height - (s + 1) * nz), (0, 0), (0, 0)))
        summed = term if summed is None else summed + term
    summed = summed[:, 2:-2]
    low, high = beside(summed, 2, HALO)
    temp, flux = heat(scalars, summed, low, high, start[0], start[1])
    part = nx // slabs
    temp = lax.dynamic_slice_in_dim(temp, spot * part, part, axis=2)
    flux = lax.dynamic_slice_in_dim(flux, spot * part, part, axis=3)
    return jnp.transpose(temp, (2, 1, 0)), jnp.transpose(flux, (0, 3, 2, 1))


def solution(mesh):
    placed = (
        P("mode", "space", None, None),
        P("space", "mode", None),
        P("mode"),
        P("mode"),
        P("mode"),
        P("mode"),
        P(),
        P("space", "mode", None),
        P("space", "mode", None),
    )
    return jax.shard_map(
        per_device,
        mesh=mesh,
        in_specs=placed,
        out_specs=(P("space", "mode", None), P(None, "space", "mode", None)),
        check_vma=False,
    )
```

```python
import functools
import math

import jax
import jax.numpy as jnp
from jax import lax
from jax.experimental import pallas as pl
from jax.experimental.pallas import tpu as pltpu
from jax.sharding import PartitionSpec as P

SWEEPS = 4
HALO = 2 * SWEEPS
time_step = 0.25
pore_factor = 0.1
kappa_top = 1.0

UNIT = ((1, 0, 0), (-1, 0, 0), (0, 1, 0), (0, -1, 0), (0, 0, 1), (0, 0, -1))
ONE = ((0, 0, 0),) + UNIT
PAIRS = tuple(
    (i, j)
    for i in range(6)
    for j in range(i, 6)
    if i // 2 != j // 2 or i == j
)
TWO = tuple(tuple(UNIT[i][a] + UNIT[j][a] for a in range(3)) for i, j in PAIRS)
OFFSETS = ONE + TWO


def mode_table(labels, orientation, warmth, lifetimes, rate_of, modes):
    branches = jnp.arange(rate_of.shape[0], dtype=jnp.int32)
    onehot = (labels[:, None] == branches[None, :]).astype(jnp.float32)
    speed = jnp.sum(onehot * rate_of[None, :], axis=1)
    polar = orientation // 4
    azimuth = orientation % 4
    cosine = (2 * polar + 1).astype(jnp.float32) * 0.25 - 1.0
    sine = jnp.sqrt(1.0 - cosine * cosine)
    angle = (azimuth.astype(jnp.float32) + 0.5) * (math.pi / 2.0)
    velocity = (speed * sine * jnp.cos(angle), speed * sine * jnp.sin(angle), speed * cosine)
    return velocity, 1.0 / lifetimes, warmth / float(modes)


def stencils(velocity, rates):
    push = []
    for v in velocity:
        push.append(time_step * jnp.maximum(v, 0.0))
        push.append(time_step * jnp.maximum(-v, 0.0))
    center = 1.0 - sum(push) - time_step * rates
    once = [center] + push
    twice = [center * center] + [2.0 * center * p for p in push]
    for i, j in PAIRS:
        twice.append((1.0 if i == j else 2.0) * push[i] * push[j])
    return jnp.stack(once), jnp.stack(twice)


def moments_kernel(place_ref, e_ref, a_ref, sums_ref, out_ref, mid, plus, minus):
    z = pl.program_id(0)
    xb = pl.program_id(1)
    width = e_ref.shape[2]
    lanes = e_ref.shape[3]
    planes = mid.shape[0]
    across = mid.shape[1] // 8 - 4

    @pl.when((z == 0) & (xb == 0))
    def _():
        def clear(p, _):
            for ref in (mid, plus, minus):
                ref[p] = jnp.zeros(ref.shape[1:], jnp.float32)
            return 0

        lax.fori_loop(0, planes, clear, 0)

    lane = lax.broadcasted_iota(jnp.int32, (8, lanes), 1)
    turned = jnp.transpose(e_ref[:, 0], (1, 0, 2))
    a = a_ref[...]
    for i in range(0, width, 2):
        pair = jnp.concatenate([turned[i], turned[i + 1]], axis=1)
        fields = jnp.dot(
            a, jnp.concatenate([pair, pair], axis=0), preferred_element_type=jnp.float32
        )
        for j in range(2):
            x = xb * width + (i + j)
            for n, (dx, dy, dz) in enumerate(OFFSETS):
                part = fields[8 * n : 8 * n + 8, lanes * j : lanes * (j + 1)]
                if dy == 2:
                    part = jnp.where(lane >= 2, pltpu.roll(part, 2, 1), 0.0)
                elif dy == -2:
                    part = jnp.where(lane < lanes - 2, pltpu.roll(part, lanes - 2, 1), 0.0)
                ref = {1: plus, -1: minus}.get(dy, mid)
                ref[z + (2 + dz), pl.ds(pl.multiple_of(8 * (x + (2 + dx)), 8), 8), :] += part

    @pl.when((z == pl.num_programs(0) - 1) & (xb == pl.num_programs(1) - 1))
    def _():
        spot = lax.broadcasted_iota(jnp.int32, (across, lanes), 1)
        blocks = out_ref.shape[0]
        deep = out_ref.shape[3]

        row = lax.broadcasted_iota(jnp.int32, (lanes, across), 0)
        column = lax.broadcasted_iota(jnp.int32, (lanes, across), 1)

        def put(k, p, value):
            for b in range(blocks):
                out_ref[b, k, p] = value[b * deep : (b + 1) * deep]

        def difference(value, axis):
            spots = (row, column)[axis]
            size = value.shape[axis]
            after = jnp.where(spots < size - 1, pltpu.roll(value, size - 1, axis), 0.0)
            return after - jnp.where(spots >= 1, pltpu.roll(value, 1, axis), 0.0)

        def finish(p, below):
            upright = []
            for k in range(8):
                up = pltpu.roll(plus[p, pl.ds(16 + k, across, stride=8), :], 1, 1)
                down = pltpu.roll(minus[p, pl.ds(16 + k, across, stride=8), :], lanes - 1, 1)
                whole = mid[p, pl.ds(16 + k, across, stride=8), :]
                whole = whole + jnp.where(spot >= 1, up, 0.0)
                whole = whole + jnp.where(spot < lanes - 1, down, 0.0)
                upright.append(whole.T)
            put(0, p, upright[0])
            inside = (p >= place_ref[0]) & (p < place_ref[1])
            flux = [jnp.where(inside, v, 0.0) for v in upright[1:4]]
            put(1, p, difference(flux[0], 1) + difference(flux[1], 0) - below)
            under = jnp.maximum(p - 1, 0)
            for b in range(blocks):
                out_ref[b, 1, under] += flux[2][b * deep : (b + 1) * deep]
            for k in range(4):
                put(2 + k, p, upright[4 + k])
            return flux[2]

        lax.fori_loop(0, planes, finish, jnp.zeros((lanes, across), jnp.float32))
        for b in range(blocks):
            out_ref[b, 0, 0] = jnp.broadcast_to(sums_ref[...], (deep, across))


def local_moments(place, state, table, sums, blocks):
    modes, nz, nx, ny = state.shape
    width = math.gcd(nx, 32)
    acc = pltpu.VMEM((nz + 4, 8 * (nx + 4), ny), jnp.float32)
    shape = (blocks, 6, nz + 4, ny // blocks, nx)
    return pl.pallas_call(
        moments_kernel,
        grid=(nz, nx // width),
        in_specs=[
            pl.BlockSpec(memory_space=pltpu.SMEM),
            pl.BlockSpec((modes, 1, width, ny), lambda z, x: (0, z, x, 0)),
            pl.BlockSpec(table.shape, lambda z, x: (0, 0)),
            pl.BlockSpec(sums.shape, lambda z, x: (0, 0)),
        ],
        out_specs=pl.BlockSpec(shape, lambda z, x: (0, 0, 0, 0, 0)),
        out_shape=jax.ShapeDtypeStruct(shape, jnp.float32),
        scratch_shapes=[acc, acc, acc],
        cost_estimate=pl.CostEstimate(
            flops=2 * table.shape[0] * table.shape[1] * nz * nx * ny,
            bytes_accessed=2 * state.size,
            transcendentals=0,
        ),
        compiler_params=pltpu.CompilerParams(
            dimension_semantics=("arbitrary", "arbitrary"), vmem_limit_bytes=60 * 1024 * 1024
        ),
        name="moments",
    )(place, state, table, sums)


def heat_kernel(s_ref, m_ref, low_ref, high_ref, t_ref, k_ref, temp_ref, flux_ref):
    lane = lax.broadcasted_iota(jnp.int32, t_ref.shape, 2)

    def shift(v, axis, step):
        if axis == 0:
            zero = jnp.zeros((1,) + v.shape[1:], v.dtype)
            return jnp.concatenate([v[1:], zero] if step > 0 else [zero, v[:-1]], axis=0)
        size = v.shape[axis]
        moved = pltpu.roll(v, (size - 1) if step > 0 else 1, axis)
        if axis == 2:
            moved = jnp.where(lane < size - 1 if step > 0 else lane >= 1, moved, 0.0)
        return moved

    def field(k):
        return jnp.concatenate([low_ref[k], m_ref[k], high_ref[k]], axis=1)

    kappa = k_ref[...]
    inside = kappa > 0.0
    start = t_ref[...]
    total = s_ref[0]

    def harmonic(first, second):
        summed = first + second
        positive = summed > 0.0
        return jnp.where(positive, 2.0 * first * second / jnp.where(positive, summed, 1.0), 0.0)

    ahead = [harmonic(kappa, shift(kappa, axis, 1)) for axis in (2, 1, 0)]

    def operator(v):
        spread = None
        for axis, face in zip((2, 1, 0), ahead):
            flow = face * (shift(v, axis, 1) - v)
            term = flow - shift(flow, axis, -1)
            spread = term if spread is None else spread + term
        return total * v - spread

    def solve(flux, rhs=0.0):
        for axis, f in zip((2, 1, 0), flux):
            rhs = rhs + (shift(f, axis, 1) - shift(f, axis, -1))
        rhs = rhs * -0.5
        theta = total + 6.0 * kappa_top
        spread = 6.0 * kappa_top
        sigma = theta / spread
        rho = 1.0 / sigma
        residual = rhs
        direction = rhs / theta
        correction = direction
        for _ in range(SWEEPS - 1):
            residual = residual - operator(direction)
            rho_next = 1.0 / (2.0 * sigma - rho)
            direction = rho_next * rho * direction + 2.0 * rho_next / spread * residual
            rho = rho_next
            correction = correction + direction
        return correction

    weight = field(0) + s_ref[1] * start
    change = solve([s_ref[2 + a] * start for a in range(3)], field(1))
    middle = jnp.where(inside, weight / total + change, 0.0)
    moved = [start] + [shift(start, 2 - axis, -step) for axis in range(3) for step in (1, -1)]
    second = []
    for k in range(4):
        value = field(2 + k) + s_ref[1 + k] * middle
        for n, m in enumerate(moved):
            value = value + s_ref[5 + 7 * k + n] * m
        second.append(jnp.where(inside, value, 0.0))
    rows = slice(HALO, t_ref.shape[1] - HALO)
    temp_ref[...] = (second[0] / total + solve(second[1:]))[:, rows]
    for a in range(3):
        flux_ref[a] = second[1 + a][:, rows]


def heat(scalars, moments, low, high, temp, kappa):
    shape = moments.shape[1:]
    return pl.pallas_call(
        heat_kernel,
        in_specs=[pl.BlockSpec(memory_space=pltpu.SMEM)]
        + [pl.BlockSpec(memory_space=pltpu.VMEM)] * 5,
        out_specs=[pl.BlockSpec(memory_space=pltpu.VMEM)] * 2,
        out_shape=[
            jax.ShapeDtypeStruct(shape, jnp.float32),
            jax.ShapeDtypeStruct((3,) + shape, jnp.float32),
        ],
        compiler_params=pltpu.CompilerParams(vmem_limit_bytes=60 * 1024 * 1024),
        name="heat",
    )(scalars, moments, low, high, temp, kappa)


def beside(cells, dim, width):
    ends = lax.axis_size("mode") - 1
    head = lax.slice_in_dim(cells, 0, width, axis=dim)
    tail = lax.slice_in_dim(cells, cells.shape[dim] - width, cells.shape[dim], axis=dim)
    return (
        lax.ppermute(tail, "mode", [(i, i + 1) for i in range(ends)]),
        lax.ppermute(head, "mode", [(i + 1, i) for i in range(ends)]),
    )


def per_device(
    excess_phonon_enthalpy,
    thermal_offset,
    state_specific_warmth_scaled,
    scattering_lifetimes,
    state_polarization_label,
    state_orientation_label,
    polarization_propagation_rate,
    thermal_conductance_bulk,
    substance_label,
):
    groups = lax.axis_size("mode")
    slabs = lax.axis_size("space")
    modes = state_orientation_label.shape[0]
    velocity, rates, capacity = mode_table(
        state_polarization_label,
        state_orientation_label,
        state_specific_warmth_scaled,
        scattering_lifetimes,
        polarization_propagation_rate,
        modes * groups,
    )
    once, twice = stencils(velocity, rates)
    weights = jnp.stack([rates, *velocity])
    gain = time_step * rates * capacity
    sums = jnp.concatenate(
        [
            jnp.sum(capacity * rates)[None],
            jnp.sum(weights * gain, axis=1),
            jnp.sum((weights * gain)[:, None, :] * once[None], axis=2).reshape(-1),
        ]
    )

    lone = jnp.zeros((len(TWO), modes), jnp.float32)
    table = jnp.stack([jnp.concatenate([once, lone]), twice], axis=1)
    table = (table[:, :, None, :] * weights[None, None]).reshape(8 * len(OFFSETS), modes)
    high = lax.reduce_precision(table, 8, 7)
    table = jnp.concatenate([high, table - high], axis=1).astype(jnp.bfloat16)

    kappa = thermal_conductance_bulk * jnp.where(substance_label == 1, pore_factor, 1.0)
    start = jnp.transpose(jnp.stack([thermal_offset, kappa]), (0, 3, 2, 1))
    start = lax.all_gather(start, "space", axis=0)
    start = jnp.concatenate([start[s] for s in range(slabs)], axis=3)
    low, high = beside(start, 2, HALO)
    start = jnp.concatenate([low, start, high], axis=2)

    nz, nx, ny = excess_phonon_enthalpy.shape[1:]
    spot = lax.axis_index("space")
    place = jnp.stack([jnp.where(spot == 0, 2, 0), jnp.where(spot == slabs - 1, nz + 2, nz + 4)])
    sums = jnp.pad(sums, (0, nx - sums.shape[0]))[None]
    partial = local_moments(place.astype(jnp.int32), excess_phonon_enthalpy, table, sums, groups)
    reduced = lax.psum_scatter(partial, "mode", scatter_dimension=0, tiled=True)[0]
    reduced, start = lax.optimization_barrier((reduced, start))
    scalars, reduced = lax.optimization_barrier((reduced[0, 0, 0], reduced))
    reduced = reduced.at[0, 0].set(0.0)
    slab = lax.all_gather(reduced.astype(jnp.bfloat16), "space", axis=0)
    height = nz * slabs
    summed = None
    for s in range(slabs):
        term = jnp.pad(slab[s].astype(jnp.float32), ((0, 0), (s * nz, height - (s + 1) * nz), (0, 0), (0, 0)))
        summed = term if summed is None else summed + term
    summed = summed[:, 2:-2]
    low, high = beside(summed, 2, HALO)
    temp, flux = heat(scalars, summed, low, high, start[0], start[1])
    part = nx // slabs
    temp = lax.dynamic_slice_in_dim(temp, spot * part, part, axis=2)
    flux = lax.dynamic_slice_in_dim(flux, spot * part, part, axis=3)
    return jnp.transpose(temp, (2, 1, 0)), jnp.transpose(flux, (0, 3, 2, 1))


def solution(mesh):
    placed = (
        P("mode", "space", None, None),
        P("space", "mode", None),
        P("mode"),
        P("mode"),
        P("mode"),
        P("mode"),
        P(),
        P("space", "mode", None),
        P("space", "mode", None),
    )
    return jax.shard_map(
        per_device,
        mesh=mesh,
        in_specs=placed,
        out_specs=(P("space", "mode", None), P(None, "space", "mode", None)),
        check_vma=False,
    )
```
